32 devices in a mesh: seq: 8 (over y, x, core), head: 4 (over z).
Axes of the slice: x: 2, y: 2, z: 4, core: 2. Of those that a mesh axis runs over, the one named last changes fastest.
Arguments:
- queries: bfloat16 [2048, 16, 128], P('seq', 'head'), may hold values from -30 to 30
- keys: bfloat16 [2048, 16, 128], P('seq', 'head'), may hold values from -12 to 12
- values: bfloat16 [2048, 16, 128], P('seq', 'head'), may hold values from -6 to 6
- log_forget: float32 [16, 2048], P('head', 'seq'), may hold values from -1.6 to 0
- strength: float32 [16, 2048], P('head', 'seq'), may hold values from 0.05 to 1
- out_weight: bfloat16 [2048, 2048], P('head'), may hold values from -0.125 to 0.125
Outputs:
- mixed: bfloat16 [2048, 2048], P(('seq', 'head'))
The draws below stay inside these ranges and needn't reach their ends.
All inputs are finite; a program needn't handle non-finite values.
Results may differ from the reference program's by a relative error of at most 0.018.
Values may be sent and summed in bfloat16 or wider, within the bound.
A program may use at most 64 MiB of HBM per device.

```python
import math
import jax
import jax.numpy as jnp
from jax import lax

D = 2048
HEADS = 16
E = 128
WINDOW = 1024
CG_STEPS = 6
SEQUENCE_TOKENS = 2048


def paired(key):
    drawn_keys = jnp.clip(jax.random.normal(jax.random.fold_in(key, 101), (SEQUENCE_TOKENS, HEADS, E), jnp.float32), -6.0, 6.0)
    drawn_queries = jnp.clip(jax.random.normal(jax.random.fold_in(key, 102), (SEQUENCE_TOKENS, HEADS, E), jnp.float32), -6.0, 6.0)
    return (drawn_queries, drawn_keys)


def draw_queries(key, part):
    return paired(key)[0].astype(jnp.bfloat16)


def draw_keys(key, part):
    return paired(key)[1].astype(jnp.bfloat16)


def draw_log_forget(key, part):
    fast = jax.random.randint(jax.random.fold_in(key, 201), (HEADS,), 0, 2) == 1
    fast_rate = 1.0 / 40.0 * jnp.exp(jax.random.uniform(jax.random.fold_in(key, 202), (HEADS,), jnp.float32, -0.29, 0.29))
    slow_rate = 0.25 / SEQUENCE_TOKENS * jnp.exp(jax.random.uniform(jax.random.fold_in(key, 203), (HEADS,), jnp.float32, -0.7, 0.7))
    learning_rate = jnp.where(fast, fast_rate, slow_rate)[:, None]
    coarse_estimate = jax.random.uniform(jax.random.fold_in(key, 204), (HEADS, SEQUENCE_TOKENS), jnp.float32, 0.5, 1.5)
    table = jnp.exp(jax.random.uniform(jax.random.fold_in(key, 205), (SEQUENCE_TOKENS // 64 + 1,), jnp.float32, -0.7, 0.7))
    block_multiplier = table[jnp.arange(SEQUENCE_TOKENS) // 64]
    spike_position = jax.random.randint(jax.random.fold_in(key, 206), (2,), 0, SEQUENCE_TOKENS)
    training_loss = jax.random.uniform(jax.random.fold_in(key, 207), (HEADS, 2), jnp.float32, 0.2, 0.5)
    match_count = (jnp.arange(SEQUENCE_TOKENS)[None, :] == spike_position[:, None]).astype(jnp.float32)
    spike_events = jnp.dot(jnp.log1p(-training_loss), match_count)
    return -learning_rate * coarse_estimate * block_multiplier[None, :] + spike_events


def shard_levels(key, dims, pieces, least, high):
    level = 1.0
    for dim, shards_of in pieces:
        draws = jax.random.uniform(jax.random.fold_in(jax.random.fold_in(key, 6), dim), (shards_of,), jnp.float32, least / len(pieces), high / len(pieces))
        level = level * jnp.repeat(jnp.exp(draws), dims[dim] // shards_of).reshape((-1,) + (1,) * (len(dims) - 1 - dim))
    return level


def centred(key, extent, scale, bound, pieces=(), kind=jnp.bfloat16):
    factor_of = shard_levels(key, extent, pieces, -0.22, 0.18) if pieces else 1.0
    result = jax.random.normal(key, extent, jnp.float32) * scale * factor_of
    return jnp.minimum(jnp.maximum(result, -bound), bound).astype(kind)


def setup_inputs(seed: int = 0) -> dict:
    key_of = jax.random.split(jax.random.key(seed), 7)
    return {
        "queries": draw_queries(jax.random.fold_in(key_of[6], 71), 0),
        "keys": draw_keys(jax.random.fold_in(key_of[6], 71), 0),
        "values": centred(key_of[2], (SEQUENCE_TOKENS, HEADS, E), 1.0, 6.0, ((0, 8), (1, 4))),
        "log_forget": draw_log_forget(jax.random.fold_in(key_of[6], 71), 0),
        "strength": jnp.clip(jnp.exp(math.log(1.0) - 2.9957323 * jax.random.uniform(key_of[4], (HEADS, SEQUENCE_TOKENS), jnp.float32) ** shard_levels(key_of[4], (HEADS, SEQUENCE_TOKENS), ((0, 4), (1, 8)), -0.2, 0.2)), 0.05, 1.0),
        "out_weight": centred(key_of[5], (HEADS * E, D), (HEADS * E) ** -0.5, 0.125, ((0, 4),)),
    }


ridge = 0.25
highest = lax.Precision.HIGHEST
tiny_floor = 1e-30

def window_attention(query_rows, key_rows, value_rows, offset):
    count = query_rows.shape[0]
    block = min(512, count)
    reach = WINDOW + block
    scale = query_rows.shape[2] ** (-0.5)
    results = []
    for block_start in range(0, count, block):
        query_block = query_rows[block_start:block_start + block].astype(jnp.float32)
        key_block = key_rows[block_start:block_start + reach].astype(jnp.float32)
        value_block = value_rows[block_start:block_start + reach].astype(jnp.float32)
        query_pos = block_start + jnp.arange(block)
        key_pos = block_start - WINDOW + jnp.arange(reach)
        admitted = (key_pos[None, :] <= query_pos[:, None]) & (key_pos[None, :] > query_pos[:, None] - WINDOW) & (key_pos[None, :] + offset >= 0)
        scores = jnp.einsum('qhe,khe->hqk', query_block, key_block, precision=highest) * scale
        scores = jnp.where(admitted[None], scores, -jnp.inf)
        largest = lax.optimization_barrier(jnp.max(scores, axis=-1, keepdims=True))
        expo = jnp.exp(scores - largest)
        weights = (expo / lax.optimization_barrier(jnp.sum(expo, axis=-1, keepdims=True))).astype(jnp.bfloat16)
        results.append(jnp.einsum('hqk,khe->qhe', weights.astype(jnp.float32), value_block, precision=highest))
    return jnp.concatenate(results, axis=0)

def group_step(state, inputs):
    key_state, value_state = state
    query_part, key_part, value_part, forget_part, strength_part = inputs
    decay_sum = jnp.cumsum(forget_part, axis=1)
    length = forget_part.shape[1]
    order = jnp.arange(length)
    causal = (order[:, None] >= order[None, :])[None]
    gap = jnp.where(causal, decay_sum[:, :, None] - decay_sum[:, None, :], 0.0)
    mixing = jnp.where(causal, jnp.exp(gap), 0.0) * strength_part[:, None, :]
    leading = jnp.exp(decay_sum)[:, :, None]

    def operator(vector):
        correlation = jnp.einsum('htf,hsf->hts', vector, key_part, precision=highest)
        carried = jnp.einsum('htf,hef->hte', vector, key_state, precision=highest)
        inside = jnp.einsum('hts,hse->hte', mixing * correlation, key_part, precision=highest)
        return leading * carried + inside + ridge * vector
    solution = jnp.zeros_like(query_part)
    residual = query_part
    direction = query_part
    norm_now = lax.optimization_barrier(jnp.sum(residual * residual, axis=-1, keepdims=True))
    for iteration in range(CG_STEPS):
        image = operator(direction)
        alpha = norm_now / jnp.maximum(lax.optimization_barrier(jnp.sum(direction * image, axis=-1, keepdims=True)), tiny_floor)
        solution = solution + alpha * direction
        residual = residual - alpha * image
        norm_next = lax.optimization_barrier(jnp.sum(residual * residual, axis=-1, keepdims=True))
        direction = residual + norm_next / jnp.maximum(norm_now, tiny_floor) * direction
        norm_now = norm_next
    correlation = jnp.einsum('htf,hsf->hts', solution, key_part, precision=highest)
    output = leading * jnp.einsum('htf,hef->hte', solution, value_state, precision=highest)
    output = output + jnp.einsum('hts,hse->hte', mixing * correlation, value_part, precision=highest)
    tail = jnp.exp(decay_sum[:, -1:] - decay_sum) * strength_part
    end_factor = jnp.exp(decay_sum[:, -1])[:, None, None]
    key_state = end_factor * key_state + jnp.einsum('hse,hsf->hef', tail[:, :, None] * key_part, key_part, precision=highest)
    value_state = end_factor * value_state + jnp.einsum('hse,hsf->hef', tail[:, :, None] * value_part, key_part, precision=highest)
    return ((key_state, value_state), output)

def normalized(rows):
    wide = rows.astype(jnp.float32)
    return wide * lax.rsqrt(lax.optimization_barrier(jnp.sum(wide * wide, axis=-1, keepdims=True)) + 1e-06)

def mesa_heads(query_rows, key_rows, value_rows, log_forget, strength, key_start, value_start):
    heads_here, count, width = query_rows.shape
    group = min(256, count)
    blocks = count // group

    def blocked(array):
        shaped = array.reshape((heads_here, blocks, group) + array.shape[2:])
        return jnp.moveaxis(shaped, 1, 0)
    inputs = (blocked(query_rows), blocked(key_rows), blocked(value_rows), blocked(log_forget), blocked(strength))
    final, outputs = lax.scan(group_step, (key_start, value_start), inputs)
    return jnp.moveaxis(outputs, 0, 1).reshape(heads_here, count, width)

def reference(queries, keys, values, log_forget, strength, out_weight):
    padding = jnp.zeros((WINDOW, HEADS, E), jnp.bfloat16)
    attended = window_attention(queries, jnp.concatenate((padding, keys), 0), jnp.concatenate((padding, values), 0), 0)
    query_norm = jnp.transpose(normalized(queries), (1, 0, 2))
    key_norm = jnp.transpose(normalized(keys), (1, 0, 2))
    value_wide = jnp.transpose(values.astype(jnp.float32), (1, 0, 2))
    empty = jnp.zeros((HEADS, E, E), jnp.float32)
    mesa = mesa_heads(query_norm, key_norm, value_wide, log_forget, strength, empty, empty)
    head_out = (attended + jnp.transpose(mesa, (1, 0, 2))).astype(jnp.bfloat16)
    flat = head_out.reshape(SEQUENCE_TOKENS, HEADS * E)
    return jnp.dot(flat, out_weight, preferred_element_type=jnp.float32).astype(jnp.bfloat16)
```

```python
import functools

import jax
import jax.numpy as jnp
from jax import lax
from jax.experimental import pallas as pl
from jax.experimental.pallas import tpu as pltpu
from jax.sharding import PartitionSpec as P

WINDOW = 1024
CG_STEPS = 6
RIDGE = 0.25
TINY = 1e-30
LOW = -1e30
MESH = pl.DeviceIdType.MESH
F32 = jnp.float32
BF16 = jnp.bfloat16


def dot(a, b):
    return lax.dot_general(a, b, (((1,), (0,)), ((), ())), preferred_element_type=F32)


def dot_t(a, b):
    return lax.dot_general(a, b, (((1,), (1,)), ((), ())), preferred_element_type=F32)


def dot_tl(a, b):
    return lax.dot_general(a, b, (((0,), (0,)), ((), ())), preferred_element_type=F32)


def split(x):
    hi = x.astype(BF16)
    return hi, (x - hi.astype(F32)).astype(BF16)


def kernel(
    n, nz, back,
    qkv_ref, fs_ref, w_hbm, out_ref,
    kv, qb, fs, st, stl, w, kk, mix, sk, sv, xs, rs, ds, nrm, att, hout, hother, rsend, lsend, rrecv, lrecv,
    w_sem, kv_s, kv_r, sib_s, q_r, fs_s, fs_r, st_s, st_r, h_sem, rs_s, rs_r, ls_s, ls_r,
):
    me = lax.axis_index("seq")
    z = lax.axis_index("head")
    chip, core = me // 2, me % 2
    sib = chip * 2 + (1 - core)
    chips = n // 2
    window = 2 * back
    half, tok, width = kv.shape[2], kv.shape[3], kv.shape[4]
    far_max = max(n - 2 * (back + 1), 0)

    def dev(s, h):
        return (s, h)

    w_copy = pltpu.make_async_copy(w_hbm, w, w_sem)
    w_copy.start()

    barrier = pltpu.get_barrier_semaphore()
    for k in range(1, n):
        pl.semaphore_signal(barrier, inc=1, device_id=dev((me + k) % n, z), device_id_type=MESH)
    for k in range(1, nz):
        pl.semaphore_signal(barrier, inc=1, device_id=dev(me, (z + k) % nz), device_id_type=MESH)
    pl.semaphore_wait(barrier, n - 1 + nz - 1)

    def remote(src, dst, s_sem, r_sem, s, h):
        return pltpu.make_async_remote_copy(
            src_ref=src, dst_ref=dst, send_sem=s_sem, recv_sem=r_sem,
            device_id=dev(s, h), device_id_type=MESH)

    def fs_copy(j, owner):
        return remote(fs_ref.at[j % 2], fs.at[owner], fs_s.at[j], fs_r.at[owner], j, z)

    for j in range(n):
        @pl.when((j // 2 >= chip) & (j != me))
        def _():
            fs_copy(j, me).start()

    def sib_copies():
        other = 1 - core
        return (
            remote(qkv_ref.at[other, pl.ds(1, 2)], kv.at[window + core], sib_s.at[0], kv_r.at[window + core], sib, z),
            remote(qkv_ref.at[other, 0], qb.at[core], sib_s.at[1], q_r, sib, z),
        )

    for c in sib_copies():
        c.start()

    def halo_copy(d, h, slot):
        return remote(qkv_ref.at[h, pl.ds(1, 2)], kv.at[slot], kv_s.at[d - 1, h], kv_r.at[slot],
                      (chip + d) * 2 + h, z)

    for d in range(1, back + 1):
        @pl.when(chip + d < chips)
        def _():
            for h in range(2):
                halo_copy(d, h, window - 2 * d + core).start()

    row = lax.broadcasted_iota(jnp.int32, (tok, tok), 0)
    col = lax.broadcasted_iota(jnp.int32, (tok, tok), 1)
    tri = row >= col
    eye = row == col

    def to_col(r):
        return jnp.sum(jnp.where(eye, jnp.broadcast_to(r, (tok, tok)), 0.0), axis=1, keepdims=True)

    def to_row(c):
        return jnp.sum(jnp.where(eye, jnp.broadcast_to(c, (tok, tok)), 0.0), axis=0, keepdims=True)

    def sums_col(r):
        return jnp.sum(jnp.where(tri, jnp.broadcast_to(r, (tok, tok)), 0.0), axis=1, keepdims=True)

    def inv_norm(x):
        x = x.astype(F32)
        return lax.rsqrt(jnp.sum(x * x, axis=-1, keepdims=True) + 1e-6)

    def local_state(k, v, f, s):
        tail = jnp.exp(jnp.sum(f, axis=1, keepdims=True) - sums_col(f)) * to_col(s)
        r = inv_norm(k)
        wk = (tail * r) * k.astype(F32)
        h0, l0 = split(wk * r)
        h1, l1 = split(wk)
        key = dot_tl(h0, k) + dot_tl(l0, k)
        val = dot_tl(h1, v) + dot_tl(l1, v)
        return key, val

    def st_copy(j, owner):
        return remote(stl.at[j % 2], st.at[owner], st_s.at[j], st_r.at[owner], j, z)

    if far_max > 0:
        @pl.when(chip + back + 1 < chips)
        def _():
            for g in range(2):
                for h in range(half):
                    a, b = local_state(qkv_ref[g, 1, h], qkv_ref[g, 2, h],
                                       fs_ref[g, h:h + 1, :], fs_ref[g, half + h:half + h + 1, :])
                    stl[g, 0, h] = a.astype(BF16)
                    stl[g, 1, h] = b.astype(BF16)
            for j in range(2 * (back + 1), n):
                @pl.when(j // 2 > chip + back)
                def _():
                    st_copy(j, me).start()

    kv[window + core] = qkv_ref[core, 1:3]
    qb[core] = qkv_ref[core, 0]
    fs[me] = fs_ref[core]

    for c in sib_copies():
        c.wait_send()
    remote(qkv_ref.at[0, pl.ds(1, 2)], kv.at[window + 1 - core], sib_s.at[0], kv_r.at[window + 1 - core], sib, z).wait_recv()
    remote(qkv_ref.at[0, 0], qb.at[1 - core], sib_s.at[1], q_r, sib, z).wait_recv()
    for j in range(n):
        @pl.when((j // 2 <= chip) & (j != me))
        def _():
            fs_copy(me, j).wait_recv()

        @pl.when((j // 2 >= chip) & (j != me))
        def _():
            fs_copy(j, me).wait_send()

    def gates(shard, h):
        at = (shard + n) % n
        both = fs[at]
        return both[h:h + 1, :], both[half + h:half + h + 1, :]

    for b in range(2):
        for h in range(half):
            i = b * half + h
            f, s = gates(chip * 2 + b, h)
            k = kv[window + b, 0, h]
            c_col = sums_col(f)
            c_row = to_row(c_col)
            r_row = to_row(inv_norm(k))
            mix[i] = jnp.where(tri, jnp.exp(jnp.minimum(c_col - c_row, 0.0)), 0.0) * (s * r_row * r_row)
            kk[i] = jnp.concatenate((k, k), axis=1)
            nrm[i] = jnp.broadcast_to(1.0 / r_row, (8, tok))
            q = qb[b, h].astype(F32)
            ds[i] = q * lax.rsqrt(jnp.sum(q * q, axis=-1, keepdims=True) + 1e-6)
            rs[i] = ds[i]
            xs[i] = jnp.zeros((tok, width), F32)

    for d in range(back, 0, -1):
        for g in range(2):
            slot = window - 2 * d + g

            @pl.when(chip >= d)
            def _():
                remote(qkv_ref.at[0, pl.ds(1, 2)], kv.at[slot], kv_s.at[0, 0], kv_r.at[slot], me, z).wait_recv()

            @pl.when(chip < d)
            def _():
                kv[slot] = jnp.zeros((2, half, tok, width), BF16)

    for j in range(far_max):
        @pl.when(j // 2 < chip - back)
        def _():
            remote(stl.at[0], st.at[j], st_s.at[0], st_r.at[j], me, z).wait_recv()

    for h in range(half):
        key = jnp.zeros((width, width), F32)
        val = jnp.zeros((width, width), F32)
        for j in range(far_max):
            ok = j // 2 < chip - back
            f, s = gates(j, h)
            e = jnp.exp(jnp.sum(f, axis=1, keepdims=True))
            key = jnp.where(ok, e * key + st[j, 0, h].astype(F32), key)
            val = jnp.where(ok, e * val + st[j, 1, h].astype(F32), val)
        for j in range(window + 1):
            ok = chip * 2 + j >= window
            f, s = gates(chip * 2 - window + j, h)
            if j == window:
                sk[h, 0], sk[h, 1] = split(key)
                sv[h, 0], sv[h, 1] = split(val)
            a, b = local_state(kv[j, 0, h], kv[j, 1, h], f, s)
            e = jnp.exp(jnp.sum(f, axis=1, keepdims=True))
            key = jnp.where(ok, e * key + a, key)
            val = jnp.where(ok, e * val + b, val)
        sk[half + h, 0], sk[half + h, 1] = split(key)
        sv[half + h, 0], sv[half + h, 1] = split(val)

    scale = width ** (-0.5)
    for b in range(2):
        for h in range(half):
            q = qb[b, h]
            parts = []
            for j in range(window + 1):
                sc = dot_t(q, kv[b + j, 0, h]) * scale
                ok = chip * 2 + b + j >= window
                if j == 0:
                    sc = jnp.where((col > row) & ok, sc, LOW)
                elif j == window:
                    sc = jnp.where(tri, sc, LOW)
                else:
                    sc = jnp.where(ok, sc, LOW)
                parts.append(sc)
            top = functools.reduce(jnp.maximum, parts)
            top = jnp.max(top, axis=1, keepdims=True)
            total = jnp.zeros((tok, tok), F32)
            acc = jnp.zeros((tok, width), F32)
            for j in range(window + 1):
                e = jnp.exp(parts[j] - top)
                total = total + e
                acc = acc + dot(e.astype(BF16), kv[b + j, 1, h])
            att[b * half + h] = acc / jnp.sum(total, axis=1, keepdims=True)

    chains = 2 * half

    def carried(i, dh, dl, ref):
        hi, lo = ref[i, 0], ref[i, 1]
        return dot(dh, hi) + dot(dl, hi) + dot(dh, lo)

    leads = []
    for b in range(2):
        for h in range(half):
            f, s = gates(chip * 2 + b, h)
            leads.append(jnp.exp(sums_col(f)))

    def step(_, carry):
        norms = []
        for i in range(chains):
            now = carry[i]
            dirn = ds[i]
            dh, dl = split(dirn)
            corr = dot_t(jnp.concatenate((dh, dl), axis=1), kk[i])
            ph, plo = split(mix[i] * corr)
            k = kk[i][:, :width]
            image = leads[i] * carried(i, dh, dl, sk) + (dot(ph, k) + dot(plo, k)) + RIDGE * dirn
            alpha = now / jnp.maximum(jnp.sum(dirn * image, axis=-1, keepdims=True), TINY)
            xs[i] = xs[i] + alpha * dirn
            res = rs[i] - alpha * image
            rs[i] = res
            new = jnp.sum(res * res, axis=-1, keepdims=True)
            ds[i] = res + (new / jnp.maximum(now, TINY)) * dirn
            norms.append(new)
        return tuple(norms)

    start = tuple(jnp.sum(ds[i] * ds[i], axis=-1, keepdims=True) for i in range(chains))
    lax.fori_loop(0, CG_STEPS, step, start)

    for b in range(2):
        for h in range(half):
            i = b * half + h
            xh, xl = split(xs[i])
            corr = dot_t(jnp.concatenate((xh, xl), axis=1), kk[i])
            ph, plo = split((mix[i] * nrm[i][0:1, :]) * corr)
            v = kv[window + b, 1, h]
            mesa = leads[i] * carried(i, xh, xl, sv) + (dot(ph, v) + dot(plo, v))
            hout[b, :, h * width:(h + 1) * width] = (att[i] + mesa).astype(BF16)

    swap = remote(hout.at[1 - core], hother, h_sem.at[0], h_sem.at[1], sib, z)
    swap.start()
    w_copy.wait()
    swap.wait()

    chunk = tok // nz
    rows = half * width

    def partial(d):
        own = hout[core, d * chunk:(d + 1) * chunk, :]
        other = hother[d * chunk:(d + 1) * chunk, :]
        return dot(own, w[core]) + dot(other, w[1 - core])

    def right(d):
        return remote(rsend.at[d], rrecv.at[d], rs_s.at[d], rs_r.at[d], me, (z + 1) % nz)

    def left(d):
        return remote(lsend.at[d], lrecv.at[d], ls_s.at[d], ls_r.at[d], me, (z + nz - 1) % nz)

    for k in range(nz - 1):
        d = nz - 1 - k

        @pl.when(z < d)
        def _():
            rsend[d] = partial(d).astype(BF16)

            @pl.when(z > 0)
            def _():
                right(d).wait_recv()
                rsend[d] = (rsend[d].astype(F32) + rrecv[d].astype(F32)).astype(BF16)

            right(d).start()

        e = k

        @pl.when(z > e)
        def _():
            lsend[e] = partial(e).astype(BF16)

            @pl.when(z < nz - 1)
            def _():
                left(e).wait_recv()
                lsend[e] = (lsend[e].astype(F32) + lrecv[e].astype(F32)).astype(BF16)

            left(e).start()

    for d in range(nz):
        @pl.when(z == d)
        def _():
            total = partial(d)
            if d > 0:
                right(d).wait_recv()
                total = total + rrecv[d].astype(F32)
            if d < nz - 1:
                left(d).wait_recv()
                total = total + lrecv[d].astype(F32)
            out_ref[...] = total.astype(BF16)

    for d in range(nz):
        @pl.when(z < d)
        def _():
            right(d).wait_send()

        @pl.when(z > d)
        def _():
            left(d).wait_send()

    for d in range(1, back + 1):
        @pl.when(chip + d < chips)
        def _():
            for h in range(2):
                halo_copy(d, h, window - 2 * d + core).wait_send()
    if far_max > 0:
        for j in range(2 * (back + 1), n):
            @pl.when(j // 2 > chip + back)
            def _():
                st_copy(j, me).wait_send()


def on_device(queries, keys, values, log_forget, strength, out_weight):
    tok, heads, width = queries.shape
    n, nz = lax.axis_size("seq"), lax.axis_size("head")
    half = heads // 2
    back = max(WINDOW // (2 * tok), 1)
    qkv = jnp.stack((queries, keys, values)).reshape(3, tok, 2, half, width)
    qkv = jnp.transpose(qkv, (2, 0, 3, 1, 4))
    fs = jnp.concatenate((log_forget.reshape(2, half, tok), strength.reshape(2, half, tok)), axis=1)
    model = out_weight.shape[1]
    weight = out_weight.reshape(2, half * width, model)
    chunk = tok // nz
    slots = 2 * back + 2
    chains = 2 * half
    far = max(n - 2 * (back + 1), 1)
    dma = pltpu.SemaphoreType.DMA
    vmem = pl.BlockSpec(memory_space=pltpu.VMEM)
    return pl.pallas_call(
        functools.partial(kernel, n, nz, back),
        out_shape=jax.ShapeDtypeStruct((chunk, model), BF16),
        in_specs=[vmem, vmem, pl.BlockSpec(memory_space=pl.ANY)],
        out_specs=vmem,
        scratch_shapes=[
            pltpu.VMEM((slots, 2, half, tok, width), BF16),
            pltpu.VMEM((2, half, tok, width), BF16),
            pltpu.VMEM((n, 2 * half, tok), F32),
            pltpu.VMEM((far, 2, half, width, width), BF16),
            pltpu.VMEM((2, 2, half, width, width), BF16),
            pltpu.VMEM((2, half * width, model), BF16),
            pltpu.VMEM((chains, tok, 2 * width), BF16),
            pltpu.VMEM((chains, tok, tok), F32),
            pltpu.VMEM((chains, 2, width, width), BF16),
            pltpu.VMEM((chains, 2, width, width), BF16),
            pltpu.VMEM((chains, tok, width), F32),
            pltpu.VMEM((chains, tok, width), F32),
            pltpu.VMEM((chains, tok, width), F32),
            pltpu.VMEM((chains, 8, tok), F32),
            pltpu.VMEM((chains, tok, width), F32),
            pltpu.VMEM((2, tok, half * width), BF16),
            pltpu.VMEM((tok, half * width), BF16),
            pltpu.VMEM((nz, chunk, model), BF16),
            pltpu.VMEM((nz, chunk, model), BF16),
            pltpu.VMEM((nz, chunk, model), BF16),
            pltpu.VMEM((nz, chunk, model), BF16),
            dma(()),
            dma((back, 2)), dma((slots,)), dma((2,)), dma(()), dma((n,)), dma((n,)),
            dma((n,)), dma((n,)), dma((2,)), dma((nz,)), dma((nz,)), dma((nz,)), dma((nz,)),
        ],
        compiler_params=pltpu.CompilerParams(
            collective_id=0, has_side_effects=True, vmem_limit_bytes=56 * 1024 * 1024),
    )(qkv, fs, weight)


def solution(mesh):
    in_specs = (
        P("seq", "head", None),
        P("seq", "head", None),
        P("seq", "head", None),
        P("head", "seq"),
        P("head", "seq"),
        P("head", None),
    )
    return jax.shard_map(
        on_device, mesh=mesh, in_specs=in_specs, out_specs=P(("seq", "head"), None), check_vma=False)
```

```python
import functools

import jax
import jax.numpy as jnp
from jax import lax
from jax.experimental import pallas as pl
from jax.experimental.pallas import tpu as pltpu
from jax.sharding import PartitionSpec as P

WINDOW = 1024
CG_STEPS = 6
RIDGE = 0.25
TINY = 1e-30
LOW = -1e30
MESH = pl.DeviceIdType.MESH
F32 = jnp.float32
BF16 = jnp.bfloat16


def dot(a, b):
    return lax.dot_general(a, b, (((1,), (0,)), ((), ())), preferred_element_type=F32)


def dot_t(a, b):
    return lax.dot_general(a, b, (((1,), (1,)), ((), ())), preferred_element_type=F32)


def dot_tl(a, b):
    return lax.dot_general(a, b, (((0,), (0,)), ((), ())), preferred_element_type=F32)


def split(x):
    hi = x.astype(BF16)
    return hi, (x - hi.astype(F32)).astype(BF16)


def kernel(
    n, nz, back,
    qkv_ref, fs_ref, w_hbm, out_ref,
    kv, qb, fs, st, stl, w, kk, mix, sk, sv, xs, rs, ds, nrm, att, hout, hother, rsend, lsend, rrecv, lrecv,
    w_sem, kv_s, kv_r, sib_s, q_r, fs_s, fs_r, st_s, st_r, rl_s, h_sem, rs_s, rs_r, ls_s, ls_r,
):
    me = lax.axis_index("seq")
    z = lax.axis_index("head")
    chip, core = me // 2, me % 2
    sib = chip * 2 + (1 - core)
    chips = n // 2
    window = 2 * back
    half, tok, width = kv.shape[2], kv.shape[3], kv.shape[4]
    far_max = max(n - 2 * (back + 1), 0)
    relay = chips == 4 and back == 2

    def dev(s, h):
        return (s, h)

    w_copy = pltpu.make_async_copy(w_hbm, w, w_sem)
    w_copy.start()

    barrier = pltpu.get_barrier_semaphore()
    for k in range(1, n):
        pl.semaphore_signal(barrier, inc=1, device_id=dev((me + k) % n, z), device_id_type=MESH)
    for k in range(1, nz):
        pl.semaphore_signal(barrier, inc=1, device_id=dev(me, (z + k) % nz), device_id_type=MESH)
    pl.semaphore_wait(barrier, n - 1 + nz - 1)

    def remote(src, dst, s_sem, r_sem, s, h):
        return pltpu.make_async_remote_copy(
            src_ref=src, dst_ref=dst, send_sem=s_sem, recv_sem=r_sem,
            device_id=dev(s, h), device_id_type=MESH)

    def fs_copy(j, owner):
        return remote(fs_ref.at[j % 2], fs.at[owner], fs_s.at[j], fs_r.at[owner], j, z)

    for j in range(n):
        @pl.when((j // 2 >= chip) & (j != me))
        def _():
            fs_copy(j, me).start()

    def sib_copies():
        other = 1 - core
        return (
            remote(qkv_ref.at[other, pl.ds(1, 2)], kv.at[window + core], sib_s.at[0], kv_r.at[window + core, 0], sib, z),
            remote(qkv_ref.at[other, 0], qb.at[core], sib_s.at[1], q_r, sib, z),
        )

    for c in sib_copies():
        c.start()

    def halo_copy(d, h, slot, part):
        return remote(qkv_ref.at[h, 1 + part], kv.at[slot, part], kv_s.at[d - 1, h, part], kv_r.at[slot, part],
                      (chip + d) * 2 + h, z)

    def halo_each(part, act):
        for d in range(back, 0, -1):
            ok = chip + d < chips
            if relay and part == 0 and d == 1:
                ok = ok & (chip != 1)

            @pl.when(ok)
            def _():
                for h in range(2):
                    act(halo_copy(d, h, window - 2 * d + core, part))

    def relay_copy(g):
        return remote(kv.at[g, 0], kv.at[window - 2 + g, 0], rl_s.at[g], kv_r.at[window - 2 + g, 0], me - 2, z)

    halo_each(0, lambda c: c.start())

    row = lax.broadcasted_iota(jnp.int32, (tok, tok), 0)
    col = lax.broadcasted_iota(jnp.int32, (tok, tok), 1)
    tri = row >= col
    eye = row == col

    def to_col(r):
        return jnp.sum(jnp.where(eye, jnp.broadcast_to(r, (tok, tok)), 0.0), axis=1, keepdims=True)

    def to_row(c):
        return jnp.sum(jnp.where(eye, jnp.broadcast_to(c, (tok, tok)), 0.0), axis=0, keepdims=True)

    def sums_col(r):
        return jnp.sum(jnp.where(tri, jnp.broadcast_to(r, (tok, tok)), 0.0), axis=1, keepdims=True)

    def inv_norm(x):
        x = x.astype(F32)
        return lax.rsqrt(jnp.sum(x * x, axis=-1, keepdims=True) + 1e-6)

    def local_state(k, v, f, s, key_too, val_too):
        tail = jnp.exp(jnp.sum(f, axis=1, keepdims=True) - sums_col(f)) * to_col(s)
        r = inv_norm(k)
        wk = (tail * r) * k.astype(F32)
        key = val = None
        if key_too:
            h0, l0 = split(wk * r)
            key = dot_tl(h0, k) + dot_tl(l0, k)
        if val_too:
            h1, l1 = split(wk)
            val = dot_tl(h1, v) + dot_tl(l1, v)
        return key, val

    def st_copy(j, owner):
        return remote(stl.at[j % 2], st.at[owner], st_s.at[j], st_r.at[owner], j, z)

    if far_max > 0:
        @pl.when(chip + back + 1 < chips)
        def _():
            for g in range(2):
                for h in range(half):
                    a, b = local_state(qkv_ref[g, 1, h], qkv_ref[g, 2, h],
                                       fs_ref[g, h:h + 1, :], fs_ref[g, half + h:half + h + 1, :], True, True)
                    stl[g, 0, h] = a.astype(BF16)
                    stl[g, 1, h] = b.astype(BF16)
            for j in range(2 * (back + 1), n):
                @pl.when(j // 2 > chip + back)
                def _():
                    st_copy(j, me).start()

    halo_each(1, lambda c: c.start())

    kv[window + core] = qkv_ref[core, 1:3]
    qb[core] = qkv_ref[core, 0]
    fs[me] = fs_ref[core]

    for c in sib_copies():
        c.wait_send()
    remote(qkv_ref.at[0, pl.ds(1, 2)], kv.at[window + 1 - core], sib_s.at[0], kv_r.at[window + 1 - core, 0], sib, z).wait_recv()
    remote(qkv_ref.at[0, 0], qb.at[1 - core], sib_s.at[1], q_r, sib, z).wait_recv()
    for j in range(n):
        @pl.when((j // 2 <= chip) & (j != me))
        def _():
            fs_copy(me, j).wait_recv()

        @pl.when((j // 2 >= chip) & (j != me))
        def _():
            fs_copy(j, me).wait_send()

    def gates(shard, h):
        at = (shard + n) % n
        both = fs[at]
        return both[h:h + 1, :], both[half + h:half + h + 1, :]

    for b in range(2):
        for h in range(half):
            i = b * half + h
            f, s = gates(chip * 2 + b, h)
            k = kv[window + b, 0, h]
            c_col = sums_col(f)
            c_row = to_row(c_col)
            r_row = to_row(inv_norm(k))
            mix[i] = jnp.where(tri, jnp.exp(jnp.minimum(c_col - c_row, 0.0)), 0.0) * (s * r_row * r_row)
            kk[i] = jnp.concatenate((k, k), axis=1)
            nrm[i] = jnp.broadcast_to(1.0 / r_row, (8, tok))
            q = qb[b, h].astype(F32)
            ds[i] = q * lax.rsqrt(jnp.sum(q * q, axis=-1, keepdims=True) + 1e-6)
            rs[i] = ds[i]
            xs[i] = jnp.zeros((tok, width), F32)

    def arrivals(part):
        for d in range(back, 0, -1):
            for g in range(2):
                slot = window - 2 * d + g

                @pl.when(chip >= d)
                def _():
                    remote(qkv_ref.at[0, 1], kv.at[slot, part], kv_s.at[0, 0, 0], kv_r.at[slot, part], me, z).wait_recv()
                    if relay and part == 0 and d == 2:
                        @pl.when(chip == 3)
                        def _():
                            relay_copy(g).start()

                @pl.when(chip < d)
                def _():
                    kv[slot, part] = jnp.zeros((half, tok, width), BF16)

    def states(part, out):
        for h in range(half):
            acc = jnp.zeros((width, width), F32)
            for j in range(far_max):
                ok = j // 2 < chip - back
                f, s = gates(j, h)
                e = jnp.exp(jnp.sum(f, axis=1, keepdims=True))
                acc = jnp.where(ok, e * acc + st[j, part, h].astype(F32), acc)
            for j in range(window + 1):
                ok = chip * 2 + j >= window
                f, s = gates(chip * 2 - window + j, h)
                if j == window:
                    out[h, 0], out[h, 1] = split(acc)
                new = local_state(kv[j, 0, h], kv[j, 1, h] if part else None, f, s, part == 0, part == 1)[part]
                e = jnp.exp(jnp.sum(f, axis=1, keepdims=True))
                acc = jnp.where(ok, e * acc + new, acc)
            out[half + h, 0], out[half + h, 1] = split(acc)

    arrivals(0)
    for j in range(far_max):
        @pl.when(j // 2 < chip - back)
        def _():
            remote(stl.at[0], st.at[j], st_s.at[0], st_r.at[j], me, z).wait_recv()
    states(0, sk)

    chains = 2 * half

    def carried(i, dh, dl, ref):
        hi, lo = ref[i, 0], ref[i, 1]
        return dot(dh, hi) + dot(dl, hi) + dot(dh, lo)

    leads = []
    for b in range(2):
        for h in range(half):
            f, s = gates(chip * 2 + b, h)
            leads.append(jnp.exp(sums_col(f)))

    def step(_, carry):
        norms = []
        for i in range(chains):
            now = carry[i]
            dirn = ds[i]
            dh, dl = split(dirn)
            corr = dot_t(jnp.concatenate((dh, dl), axis=1), kk[i])
            ph, plo = split(mix[i] * corr)
            k = kk[i][:, :width]
            image = leads[i] * carried(i, dh, dl, sk) + (dot(ph, k) + dot(plo, k)) + RIDGE * dirn
            alpha = now / jnp.maximum(jnp.sum(dirn * image, axis=-1, keepdims=True), TINY)
            xs[i] = xs[i] + alpha * dirn
            res = rs[i] - alpha * image
            rs[i] = res
            new = jnp.sum(res * res, axis=-1, keepdims=True)
            ds[i] = res + (new / jnp.maximum(now, TINY)) * dirn
            norms.append(new)
        return tuple(norms)

    start = tuple(jnp.sum(ds[i] * ds[i], axis=-1, keepdims=True) for i in range(chains))
    lax.fori_loop(0, CG_STEPS, step, start)

    arrivals(1)
    states(1, sv)

    scale = width ** (-0.5)
    for b in range(2):
        for h in range(half):
            q = qb[b, h]
            parts = []
            for j in range(window + 1):
                sc = dot_t(q, kv[b + j, 0, h]) * scale
                ok = chip * 2 + b + j >= window
                if j == 0:
                    sc = jnp.where((col > row) & ok, sc, LOW)
                elif j == window:
                    sc = jnp.where(tri, sc, LOW)
                else:
                    sc = jnp.where(ok, sc, LOW)
                parts.append(sc)
            top = functools.reduce(jnp.maximum, parts)
            top = jnp.max(top, axis=1, keepdims=True)
            total = jnp.zeros((tok, tok), F32)
            acc = jnp.zeros((tok, width), F32)
            for j in range(window + 1):
                e = jnp.exp(parts[j] - top)
                total = total + e
                acc = acc + dot(e.astype(BF16), kv[b + j, 1, h])
            att[b * half + h] = acc / jnp.sum(total, axis=1, keepdims=True)

    for b in range(2):
        for h in range(half):
            i = b * half + h
            xh, xl = split(xs[i])
            corr = dot_t(jnp.concatenate((xh, xl), axis=1), kk[i])
            ph, plo = split((mix[i] * nrm[i][0:1, :]) * corr)
            v = kv[window + b, 1, h]
            mesa = leads[i] * carried(i, xh, xl, sv) + (dot(ph, v) + dot(plo, v))
            hout[b, :, h * width:(h + 1) * width] = (att[i] + mesa).astype(BF16)

    swap = remote(hout.at[1 - core], hother, h_sem.at[0], h_sem.at[1], sib, z)
    swap.start()
    w_copy.wait()
    swap.wait()

    chunk = tok // nz
    pieces = rsend.shape[1]
    cols = w.shape[2] // pieces

    def at(p):
        return pl.ds(pl.multiple_of(p * cols, cols), cols)

    def partial(d, p):
        own = hout[core, d * chunk:(d + 1) * chunk, :]
        other = hother[d * chunk:(d + 1) * chunk, :]
        return dot(own, w[core, :, at(p)]) + dot(other, w[1 - core, :, at(p)])

    def right(d, p):
        return remote(rsend.at[d, p], rrecv.at[d, p], rs_s.at[d, p], rs_r.at[d, p], me, (z + 1) % nz)

    def left(d, p):
        return remote(lsend.at[d, p], lrecv.at[d, p], ls_s.at[d, p], ls_r.at[d, p], me, (z + nz - 1) % nz)

    for k in range(nz - 1):
        d, e = nz - 1 - k, k

        @pl.loop(0, pieces)
        def _(p):
            @pl.when(z < d)
            def _():
                @pl.when(z == 0)
                def _():
                    rsend[d, p] = partial(d, p).astype(BF16)

                @pl.when(z > 0)
                def _():
                    mine = partial(d, p)
                    right(d, p).wait_recv()
                    rsend[d, p] = (mine + rrecv[d, p].astype(F32)).astype(BF16)

                right(d, p).start()

            @pl.when(z > e)
            def _():
                @pl.when(z == nz - 1)
                def _():
                    lsend[e, p] = partial(e, p).astype(BF16)

                @pl.when(z < nz - 1)
                def _():
                    mine = partial(e, p)
                    left(e, p).wait_recv()
                    lsend[e, p] = (mine + lrecv[e, p].astype(F32)).astype(BF16)

                left(e, p).start()

    for d in range(nz):
        @pl.when(z == d)
        def _():
            @pl.loop(0, pieces)
            def _(p):
                total = partial(d, p)
                if d > 0:
                    right(d, p).wait_recv()
                    total = total + rrecv[d, p].astype(F32)
                if d < nz - 1:
                    left(d, p).wait_recv()
                    total = total + lrecv[d, p].astype(F32)
                out_ref[:, at(p)] = total.astype(BF16)

    for d in range(nz):
        for p in range(pieces):
            @pl.when(z < d)
            def _():
                right(d, p).wait_send()

            @pl.when(z > d)
            def _():
                left(d, p).wait_send()

    halo_each(0, lambda c: c.wait_send())
    halo_each(1, lambda c: c.wait_send())
    if relay:
        @pl.when(chip == 3)
        def _():
            for g in range(2):
                relay_copy(g).wait_send()
    if far_max > 0:
        for j in range(2 * (back + 1), n):
            @pl.when(j // 2 > chip + back)
            def _():
                st_copy(j, me).wait_send()


def on_device(queries, keys, values, log_forget, strength, out_weight):
    tok, heads, width = queries.shape
    n, nz = lax.axis_size("seq"), lax.axis_size("head")
    half = heads // 2
    back = max(WINDOW // (2 * tok), 1)
    qkv = jnp.stack((queries, keys, values)).reshape(3, tok, 2, half, width)
    qkv = jnp.transpose(qkv, (2, 0, 3, 1, 4))
    fs = jnp.concatenate((log_forget.reshape(2, half, tok), strength.reshape(2, half, tok)), axis=1)
    model = out_weight.shape[1]
    weight = out_weight.reshape(2, half * width, model)
    chunk = tok // nz
    slots = 2 * back + 2
    chains = 2 * half
    pieces = 4
    far = max(n - 2 * (back + 1), 1)
    dma = pltpu.SemaphoreType.DMA
    vmem = pl.BlockSpec(memory_space=pltpu.VMEM)
    return pl.pallas_call(
        functools.partial(kernel, n, nz, back),
        out_shape=jax.ShapeDtypeStruct((chunk, model), BF16),
        in_specs=[vmem, vmem, pl.BlockSpec(memory_space=pl.ANY)],
        out_specs=vmem,
        scratch_shapes=[
            pltpu.VMEM((slots, 2, half, tok, width), BF16),
            pltpu.VMEM((2, half, tok, width), BF16),
            pltpu.VMEM((n, 2 * half, tok), F32),
            pltpu.VMEM((far, 2, half, width, width), BF16),
            pltpu.VMEM((2, 2, half, width, width), BF16),
            pltpu.VMEM((2, half * width, model), BF16),
            pltpu.VMEM((chains, tok, 2 * width), BF16),
            pltpu.VMEM((chains, tok, tok), F32),
            pltpu.VMEM((chains, 2, width, width), BF16),
            pltpu.VMEM((chains, 2, width, width), BF16),
            pltpu.VMEM((chains, tok, width), F32),
            pltpu.VMEM((chains, tok, width), F32),
            pltpu.VMEM((chains, tok, width), F32),
            pltpu.VMEM((chains, 8, tok), F32),
            pltpu.VMEM((chains, tok, width), F32),
            pltpu.VMEM((2, tok, half * width), BF16),
            pltpu.VMEM((tok, half * width), BF16),
            pltpu.VMEM((nz, pieces, chunk, model // pieces), BF16),
            pltpu.VMEM((nz, pieces, chunk, model // pieces), BF16),
            pltpu.VMEM((nz, pieces, chunk, model // pieces), BF16),
            pltpu.VMEM((nz, pieces, chunk, model // pieces), BF16),
            dma(()),
            dma((back, 2, 2)), dma((slots, 2)), dma((2,)), dma(()), dma((n,)), dma((n,)),
            dma((n,)), dma((n,)), dma((2,)), dma((2,)),
            dma((nz, pieces)), dma((nz, pieces)), dma((nz, pieces)), dma((nz, pieces)),
        ],
        compiler_params=pltpu.CompilerParams(
            collective_id=0, has_side_effects=True, vmem_limit_bytes=56 * 1024 * 1024),
    )(qkv, fs, weight)


def solution(mesh):
    in_specs = (
        P("seq", "head", None),
        P("seq", "head", None),
        P("seq", "head", None),
        P("head", "seq"),
        P("head", "seq"),
        P("head", None),
    )
    return jax.shard_map(
        on_device, mesh=mesh, in_specs=in_specs, out_specs=P(("seq", "head"), None), check_vma=False)
```

```python
import functools

import jax
import jax.numpy as jnp
from jax import lax
from jax.experimental import pallas as pl
from jax.experimental.pallas import tpu as pltpu
from jax.sharding import PartitionSpec as P

WINDOW = 1024
CG_STEPS = 6
RIDGE = 0.25
TINY = 1e-30
LOW = -1e30
MESH = pl.DeviceIdType.MESH
F32 = jnp.float32
BF16 = jnp.bfloat16


def dot(a, b):
    return lax.dot_general(a, b, (((1,), (0,)), ((), ())), preferred_element_type=F32)


def dot_t(a, b):
    return lax.dot_general(a, b, (((1,), (1,)), ((), ())), preferred_element_type=F32)


def dot_tl(a, b):
    return lax.dot_general(a, b, (((0,), (0,)), ((), ())), preferred_element_type=F32)


def split(x):
    hi = x.astype(BF16)
    return hi, (x - hi.astype(F32)).astype(BF16)


def kernel(
    n, nz, back,
    q_ref, k_ref, v_ref, fs_ref, w_hbm, out_ref,
    kv, qb, fs, st, stl, w, kk, mix, sk, sv, xs, rs, ds, nrm, att, hout, hother, prt, rsend, lsend, rrecv, lrecv,
    w_sem, kv_s, kv_r, sib_s, q_r, fs_s, fs_r, st_s, st_r, rl_s, h_sem, rs_s, rs_r, ls_s, ls_r,
):
    me = lax.axis_index("seq")
    z = lax.axis_index("head")
    chip, core = me // 2, me % 2
    sib = chip * 2 + (1 - core)
    chips = n // 2
    window = 2 * back
    half, tok, width = kv.shape[2], kv.shape[3], kv.shape[4]
    far_max = max(n - 2 * (back + 1), 0)
    relay = chips == 4 and back == 2

    def dev(s, h):
        return (s, h)

    w_copy = pltpu.make_async_copy(w_hbm, w, w_sem)
    w_copy.start()

    barrier = pltpu.get_barrier_semaphore()
    for k in range(1, n):
        pl.semaphore_signal(barrier, inc=1, device_id=dev((me + k) % n, z), device_id_type=MESH)
    for k in range(1, nz):
        pl.semaphore_signal(barrier, inc=1, device_id=dev(me, (z + k) % nz), device_id_type=MESH)
    pl.semaphore_wait(barrier, n - 1 + nz - 1)

    def remote(src, dst, s_sem, r_sem, s, h):
        return pltpu.make_async_remote_copy(
            src_ref=src, dst_ref=dst, send_sem=s_sem, recv_sem=r_sem,
            device_id=dev(s, h), device_id_type=MESH)

    def fs_copy(j, owner):
        return remote(fs_ref.at[j % 2], fs.at[owner], fs_s.at[j], fs_r.at[owner], j, z)

    for j in range(n):
        @pl.when((j // 2 >= chip) & (j != me))
        def _():
            fs_copy(j, me).start()

    def sib_copies():
        other = 1 - core
        return (
            remote(k_ref.at[other], kv.at[window + core, 0], sib_s.at[0], kv_r.at[window + core, 0], sib, z),
            remote(q_ref.at[other], qb.at[core], sib_s.at[1], q_r, sib, z),
            remote(v_ref.at[other], kv.at[window + core, 1], sib_s.at[2], kv_r.at[window + core, 1], sib, z),
        )

    for c in sib_copies():
        c.start()

    def halo_copy(d, h, slot, part):
        return remote((k_ref, v_ref)[part].at[h], kv.at[slot, part], kv_s.at[d - 1, h, part], kv_r.at[slot, part],
                      (chip + d) * 2 + h, z)

    def halo_each(part, act):
        for d in range(back, 0, -1):
            ok = chip + d < chips
            if relay and part == 0 and d == 1:
                ok = ok & (chip != 1)

            @pl.when(ok)
            def _():
                for h in range(2):
                    act(halo_copy(d, h, window - 2 * d + core, part))

    def relay_copy(g):
        return remote(kv.at[g, 0], kv.at[window - 2 + g, 0], rl_s.at[g], kv_r.at[window - 2 + g, 0], me - 2, z)

    halo_each(0, lambda c: c.start())

    row = lax.broadcasted_iota(jnp.int32, (tok, tok), 0)
    col = lax.broadcasted_iota(jnp.int32, (tok, tok), 1)
    tri = row >= col
    eye = row == col

    def to_col(r):
        return jnp.sum(jnp.where(eye, jnp.broadcast_to(r, (tok, tok)), 0.0), axis=1, keepdims=True)

    def to_row(c):
        return jnp.sum(jnp.where(eye, jnp.broadcast_to(c, (tok, tok)), 0.0), axis=0, keepdims=True)

    def sums_col(r):
        return jnp.sum(jnp.where(tri, jnp.broadcast_to(r, (tok, tok)), 0.0), axis=1, keepdims=True)

    def inv_norm(x):
        x = x.astype(F32)
        return lax.rsqrt(jnp.sum(x * x, axis=-1, keepdims=True) + 1e-6)

    def local_state(k, v, f, s, key_too, val_too):
        tail = jnp.exp(jnp.sum(f, axis=1, keepdims=True) - sums_col(f)) * to_col(s)
        r = inv_norm(k)
        wk = (tail * r) * k.astype(F32)
        key = val = None
        if key_too:
            h0, l0 = split(wk * r)
            key = dot_tl(h0, k) + dot_tl(l0, k)
        if val_too:
            h1, l1 = split(wk)
            val = dot_tl(h1, v) + dot_tl(l1, v)
        return key, val

    def st_copy(j, owner):
        return remote(stl.at[j % 2], st.at[owner], st_s.at[j], st_r.at[owner], j, z)

    if far_max > 0:
        @pl.when(chip + back + 1 < chips)
        def _():
            for g in range(2):
                for h in range(half):
                    a, b = local_state(k_ref[g, h], v_ref[g, h],
                                       fs_ref[g, h:h + 1, :], fs_ref[g, half + h:half + h + 1, :], True, True)
                    stl[g, 0, h] = a.astype(BF16)
                    stl[g, 1, h] = b.astype(BF16)
            for j in range(2 * (back + 1), n):
                @pl.when(j // 2 > chip + back)
                def _():
                    st_copy(j, me).start()

    halo_each(1, lambda c: c.start())

    kv[window + core, 0] = k_ref[core]
    kv[window + core, 1] = v_ref[core]
    qb[core] = q_ref[core]
    fs[me] = fs_ref[core]

    for c in sib_copies():
        c.wait_send()
    for part in range(2):
        remote(k_ref.at[0], kv.at[window + 1 - core, part], sib_s.at[0], kv_r.at[window + 1 - core, part], sib, z).wait_recv()
    remote(q_ref.at[0], qb.at[1 - core], sib_s.at[1], q_r, sib, z).wait_recv()
    for j in range(n):
        @pl.when((j // 2 <= chip) & (j != me))
        def _():
            fs_copy(me, j).wait_recv()

        @pl.when((j // 2 >= chip) & (j != me))
        def _():
            fs_copy(j, me).wait_send()

    def gates(shard, h):
        at = (shard + n) % n
        both = fs[at]
        return both[h:h + 1, :], both[half + h:half + h + 1, :]

    for b in range(2):
        for h in range(half):
            i = b * half + h
            f, s = gates(chip * 2 + b, h)
            k = kv[window + b, 0, h]
            c_col = sums_col(f)
            c_row = to_row(c_col)
            r_row = to_row(inv_norm(k))
            mix[i] = jnp.where(tri, jnp.exp(jnp.minimum(c_col - c_row, 0.0)), 0.0) * (s * r_row * r_row)
            kk[i] = jnp.concatenate((k, k), axis=1)
            nrm[i] = jnp.broadcast_to(1.0 / r_row, (8, tok))
            q = qb[b, h].astype(F32)
            ds[i] = q * lax.rsqrt(jnp.sum(q * q, axis=-1, keepdims=True) + 1e-6)
            rs[i] = ds[i]
            xs[i] = jnp.zeros((tok, width), F32)

    def arrivals(part):
        for d in range(back, 0, -1):
            for g in range(2):
                slot = window - 2 * d + g

                @pl.when(chip >= d)
                def _():
                    remote(k_ref.at[0], kv.at[slot, part], kv_s.at[0, 0, 0], kv_r.at[slot, part], me, z).wait_recv()
                    if relay and part == 0 and d == 2:
                        @pl.when(chip == 3)
                        def _():
                            relay_copy(g).start()

                @pl.when(chip < d)
                def _():
                    kv[slot, part] = jnp.zeros((half, tok, width), BF16)

    def states(part, out):
        for h in range(half):
            acc = jnp.zeros((width, width), F32)
            for j in range(far_max):
                ok = j // 2 < chip - back
                f, s = gates(j, h)
                e = jnp.exp(jnp.sum(f, axis=1, keepdims=True))
                acc = jnp.where(ok, e * acc + st[j, part, h].astype(F32), acc)
            for j in range(window + 1):
                ok = chip * 2 + j >= window
                f, s = gates(chip * 2 - window + j, h)
                if j == window:
                    out[h, 0], out[h, 1] = split(acc)
                new = local_state(kv[j, 0, h], kv[j, 1, h] if part else None, f, s, part == 0, part == 1)[part]
                e = jnp.exp(jnp.sum(f, axis=1, keepdims=True))
                acc = jnp.where(ok, e * acc + new, acc)
            out[half + h, 0], out[half + h, 1] = split(acc)

    arrivals(0)
    for j in range(far_max):
        @pl.when(j // 2 < chip - back)
        def _():
            remote(stl.at[0], st.at[j], st_s.at[0], st_r.at[j], me, z).wait_recv()
    states(0, sk)

    chains = 2 * half

    def carried(i, dh, dl, ref):
        hi, lo = ref[i, 0], ref[i, 1]
        return dot(dh, hi) + dot(dl, hi) + dot(dh, lo)

    leads = []
    for b in range(2):
        for h in range(half):
            f, s = gates(chip * 2 + b, h)
            leads.append(jnp.exp(sums_col(f)))

    def step(_, carry):
        norms = []
        for i in range(chains):
            now = carry[i]
            dirn = ds[i]
            dh, dl = split(dirn)
            corr = dot_t(jnp.concatenate((dh, dl), axis=1), kk[i])
            ph, plo = split(mix[i] * corr)
            k = kk[i][:, :width]
            image = leads[i] * carried(i, dh, dl, sk) + (dot(ph, k) + dot(plo, k)) + RIDGE * dirn
            alpha = now / jnp.maximum(jnp.sum(dirn * image, axis=-1, keepdims=True), TINY)
            xs[i] = xs[i] + alpha * dirn
            res = rs[i] - alpha * image
            rs[i] = res
            new = jnp.sum(res * res, axis=-1, keepdims=True)
            ds[i] = res + (new / jnp.maximum(now, TINY)) * dirn
            norms.append(new)
        return tuple(norms)

    start = tuple(jnp.sum(ds[i] * ds[i], axis=-1, keepdims=True) for i in range(chains))
    lax.fori_loop(0, CG_STEPS, step, start)

    arrivals(1)
    states(1, sv)

    scale = width ** (-0.5)
    for b in range(2):
        for h in range(half):
            q = qb[b, h]
            parts = []
            for j in range(window + 1):
                sc = dot_t(q, kv[b + j, 0, h]) * scale
                ok = chip * 2 + b + j >= window
                if j == 0:
                    sc = jnp.where((col > row) & ok, sc, LOW)
                elif j == window:
                    sc = jnp.where(tri, sc, LOW)
                else:
                    sc = jnp.where(ok, sc, LOW)
                parts.append(sc)
            top = functools.reduce(jnp.maximum, parts)
            top = jnp.max(top, axis=1, keepdims=True)
            total = jnp.zeros((tok, tok), F32)
            acc = jnp.zeros((tok, width), F32)
            for j in range(window + 1):
                e = jnp.exp(parts[j] - top)
                total = total + e
                acc = acc + dot(e.astype(BF16), kv[b + j, 1, h])
            att[b * half + h] = acc / jnp.sum(total, axis=1, keepdims=True)

    for b in range(2):
        for h in range(half):
            i = b * half + h
            xh, xl = split(xs[i])
            corr = dot_t(jnp.concatenate((xh, xl), axis=1), kk[i])
            ph, plo = split((mix[i] * nrm[i][0:1, :]) * corr)
            v = kv[window + b, 1, h]
            mesa = leads[i] * carried(i, xh, xl, sv) + (dot(ph, v) + dot(plo, v))
            hout[b, :, h * width:(h + 1) * width] = (att[i] + mesa).astype(BF16)

    swap = remote(hout.at[1 - core], hother, h_sem.at[0], h_sem.at[1], sib, z)
    swap.start()
    w_copy.wait()
    prt[...] = dot(hout[core], w[core])
    swap.wait()

    chunk = tok // nz
    pieces = rsend.shape[1]
    cols = w.shape[2] // pieces

    def at(p):
        return pl.ds(pl.multiple_of(p * cols, cols), cols)

    prt[...] += dot(hother[...], w[1 - core])

    def partial(d, p):
        return prt[d * chunk:(d + 1) * chunk, at(p)]

    def right(d, p):
        return remote(rsend.at[d, p], rrecv.at[d, p], rs_s.at[d, p], rs_r.at[d, p], me, (z + 1) % nz)

    def left(d, p):
        return remote(lsend.at[d, p], lrecv.at[d, p], ls_s.at[d, p], ls_r.at[d, p], me, (z + nz - 1) % nz)

    def go_right(d):
        @pl.when(z < d)
        def _():
            @pl.loop(0, pieces)
            def _(p):
                @pl.when(z == 0)
                def _():
                    rsend[d, p] = partial(d, p).astype(BF16)

                @pl.when(z > 0)
                def _():
                    right(d, p).wait_recv()
                    rsend[d, p] = (partial(d, p) + rrecv[d, p].astype(F32)).astype(BF16)

                right(d, p).start()

    def go_left(d):
        @pl.when(z > d)
        def _():
            @pl.loop(0, pieces)
            def _(p):
                @pl.when(z == nz - 1)
                def _():
                    lsend[d, p] = partial(d, p).astype(BF16)

                @pl.when(z < nz - 1)
                def _():
                    left(d, p).wait_recv()
                    lsend[d, p] = (partial(d, p) + lrecv[d, p].astype(F32)).astype(BF16)

                left(d, p).start()

    @pl.when(z < nz // 2)
    def _():
        for k in range(nz - 1):
            go_right(nz - 1 - k)
            go_left(k)

    @pl.when(z >= nz // 2)
    def _():
        for k in range(nz - 1):
            go_left(k)
            go_right(nz - 1 - k)

    for d in range(nz):
        @pl.when(z == d)
        def _():
            @pl.loop(0, pieces)
            def _(p):
                total = partial(d, p)
                if d > 0:
                    right(d, p).wait_recv()
                    total = total + rrecv[d, p].astype(F32)
                if d < nz - 1:
                    left(d, p).wait_recv()
                    total = total + lrecv[d, p].astype(F32)
                out_ref[:, at(p)] = total.astype(BF16)

    for d in range(nz):
        for p in range(pieces):
            @pl.when(z < d)
            def _():
                right(d, p).wait_send()

            @pl.when(z > d)
            def _():
                left(d, p).wait_send()

    halo_each(0, lambda c: c.wait_send())
    halo_each(1, lambda c: c.wait_send())
    if relay:
        @pl.when(chip == 3)
        def _():
            for g in range(2):
                relay_copy(g).wait_send()
    if far_max > 0:
        for j in range(2 * (back + 1), n):
            @pl.when(j // 2 > chip + back)
            def _():
                st_copy(j, me).wait_send()


def on_device(queries, keys, values, log_forget, strength, out_weight):
    tok, heads, width = queries.shape
    n, nz = lax.axis_size("seq"), lax.axis_size("head")
    half = heads // 2
    back = max(WINDOW // (2 * tok), 1)
    by_head = [jnp.transpose(x, (1, 0, 2)).reshape(2, half, tok, width) for x in (queries, keys, values)]
    fs = jnp.concatenate((log_forget.reshape(2, half, tok), strength.reshape(2, half, tok)), axis=1)
    model = out_weight.shape[1]
    weight = out_weight.reshape(2, half * width, model)
    chunk = tok // nz
    slots = 2 * back + 2
    chains = 2 * half
    pieces = 2
    far = max(n - 2 * (back + 1), 1)
    dma = pltpu.SemaphoreType.DMA
    vmem = pl.BlockSpec(memory_space=pltpu.VMEM)
    return pl.pallas_call(
        functools.partial(kernel, n, nz, back),
        out_shape=jax.ShapeDtypeStruct((chunk, model), BF16),
        in_specs=[vmem, vmem, vmem, vmem, pl.BlockSpec(memory_space=pl.ANY)],
        out_specs=vmem,
        scratch_shapes=[
            pltpu.VMEM((slots, 2, half, tok, width), BF16),
            pltpu.VMEM((2, half, tok, width), BF16),
            pltpu.VMEM((n, 2 * half, tok), F32),
            pltpu.VMEM((far, 2, half, width, width), BF16),
            pltpu.VMEM((2, 2, half, width, width), BF16),
            pltpu.VMEM((2, half * width, model), BF16),
            pltpu.VMEM((chains, tok, 2 * width), BF16),
            pltpu.VMEM((chains, tok, tok), F32),
            pltpu.VMEM((chains, 2, width, width), BF16),
            pltpu.VMEM((chains, 2, width, width), BF16),
            pltpu.VMEM((chains, tok, width), F32),
            pltpu.VMEM((chains, tok, width), F32),
            pltpu.VMEM((chains, tok, width), F32),
            pltpu.VMEM((chains, 8, tok), F32),
            pltpu.VMEM((chains, tok, width), F32),
            pltpu.VMEM((2, tok, half * width), BF16),
            pltpu.VMEM((tok, half * width), BF16),
            pltpu.VMEM((tok, model), F32),
            pltpu.VMEM((nz, pieces, chunk, model // pieces), BF16),
            pltpu.VMEM((nz, pieces, chunk, model // pieces), BF16),
            pltpu.VMEM((nz, pieces, chunk, model // pieces), BF16),
            pltpu.VMEM((nz, pieces, chunk, model // pieces), BF16),
            dma(()),
            dma((back, 2, 2)), dma((slots, 2)), dma((3,)), dma(()), dma((n,)), dma((n,)),
            dma((n,)), dma((n,)), dma((2,)), dma((2,)),
            dma((nz, pieces)), dma((nz, pieces)), dma((nz, pieces)), dma((nz, pieces)),
        ],
        compiler_params=pltpu.CompilerParams(
            collective_id=0, has_side_effects=True, vmem_limit_bytes=56 * 1024 * 1024),
    )(*by_head, fs, weight)


def solution(mesh):
    in_specs = (
        P("seq", "head", None),
        P("seq", "head", None),
        P("seq", "head", None),
        P("head", "seq"),
        P("head", "seq"),
        P("head", None),
    )
    return jax.shard_map(
        on_device, mesh=mesh, in_specs=in_specs, out_specs=P(("seq", "head"), None), check_vma=False)
```
